32 devices in a mesh: outer: 8 (over z, x), inner: 4 (over y, core).
Axes of the slice: x: 2, y: 2, z: 4, core: 2. Of those that a mesh axis runs over, the one named last changes fastest.
Arguments:
- resid: bfloat16 [4096, 2048], P(('outer', 'inner')), may hold values from -40 to 40
- queries: bfloat16 [4096, 256], P(('outer', 'inner')), may hold values from -80 to 80
- keyvals: bfloat16 [4096, 256], P(('outer', 'inner')), may hold values from -10 to 10
- piece_order: int32 [8], replicated, may hold values from 0 to 7, each once
- out_proj: bfloat16 [256, 2048], replicated, may hold values from -0.75 to 0.75
- mlp_gain: float32 [2048], replicated, may hold values from 0.25 to 1.75
- w_gate: bfloat16 [2048, 7168], P('inner', 'outer'), may hold values from -0.125 to 0.125
- w_up: bfloat16 [2048, 7168], P('inner', 'outer'), may hold values from -0.125 to 0.125
- w_down: bfloat16 [7168, 2048], P('outer', 'inner'), may hold values from -0.0625 to 0.0625
Outputs:
- layer_out: bfloat16 [4096, 2048], P(('outer', 'inner'))
The draws below stay inside these ranges and needn't reach their ends.
Inputs may be any that keep to these rules, and one draw needn't show every extreme that they name: `piece_order`: each of the 8 piece numbers appears once.
All inputs are finite; a program needn't handle non-finite values.
Results may differ from the reference program's by a relative error of at most 0.014.
Values may be sent and summed in bfloat16 or wider, within the bound.
A program may use at most 64 MiB of HBM per device.

```python
import jax
import jax.numpy as jnp
from jax import lax

D = 2048
FF = 7168
HD = 128
QHEADS = 2
SPAN = 64
PIECES = 8
BLOCK = 512
SEQ = 4096


def attention_inputs(key):
    base_key = jax.random.fold_in(key, 7)
    query_key, key_key, value_key = jax.random.split(base_key, 3)
    queries = jnp.clip(jax.random.normal(query_key, (SEQ, QHEADS * HD), jnp.float32), -4.0, 4.0)
    key_rows = 2.5 * jnp.clip(jax.random.normal(key_key, (SEQ, HD), jnp.float32), -4.0, 4.0)
    values = jnp.clip(jax.random.normal(value_key, (SEQ, HD), jnp.float32), -4.0, 4.0)
    return (queries, jnp.concatenate([key_rows, values], 1))


def draw_queries(key, part):
    return attention_inputs(key)[0].astype(jnp.bfloat16)


def draw_keyvals(key, part):
    return attention_inputs(key)[1].astype(jnp.bfloat16)


def draw_resid(key, part):
    base_key = jax.random.fold_in(key, 11)
    normal_key = jax.random.fold_in(base_key, 0)
    values = jnp.clip(jax.random.normal(normal_key, (SEQ, D), jnp.float32), -4.0, 4.0)
    return values.astype(jnp.bfloat16)


def block_scale(rng, extent, shards, low, top_value):
    gain, own = 1.0, jax.random.fold_in(rng, 6)
    for dim, parts in shards:
        draws = jnp.exp(jax.random.uniform(jax.random.fold_in(own, dim), (parts,), jnp.float32, low / len(shards), top_value / len(shards)))
        gain = gain * jnp.repeat(draws, extent[dim] // parts).reshape([-1 if axis == dim else 1 for axis in range(len(extent))])
    return gain


def scatter_about(rng, extent, scale, reach, cuts=(), held_as=jnp.bfloat16):
    gain = block_scale(rng, extent, cuts, -0.22, 0.18) if cuts else 1.0
    entries = jax.random.normal(rng, extent, jnp.float32) * scale * gain
    return jnp.minimum(jnp.maximum(entries, -reach), reach).astype(held_as)


def setup_inputs(seed: int = 0) -> dict:
    streams_of = jax.random.split(jax.random.key(seed), 10)
    return {
        "resid": draw_resid(jax.random.fold_in(streams_of[9], 71), 0),
        "queries": draw_queries(jax.random.fold_in(streams_of[9], 71), 0),
        "keyvals": draw_keyvals(jax.random.fold_in(streams_of[9], 71), 0),
        "piece_order": jax.random.permutation(streams_of[3], PIECES).astype(jnp.int32),
        "out_proj": scatter_about(streams_of[4], (QHEADS * HD, D), 64 ** -0.5, 0.75),
        "mlp_gain": jnp.clip(1.0 + 0.15 * jax.random.normal(streams_of[5], (D,), jnp.float32), 0.25, 1.75),
        "w_gate": scatter_about(streams_of[6], (D, FF), D ** -0.5, 0.125, ((0, 4), (1, 8))),
        "w_up": scatter_about(streams_of[7], (D, FF), D ** -0.5, 0.125, ((0, 4), (1, 8))),
        "w_down": scatter_about(streams_of[8], (FF, D), FF ** -0.5, 0.0625, ((0, 8), (1, 4))),
    }


def reference(resid, queries, keyvals, piece_order, out_proj, mlp_gain, w_gate, w_up, w_down):
    block_pos = (piece_order[:, None] * SPAN + jnp.arange(SPAN, dtype=jnp.int32)[None, :]).reshape(BLOCK)
    block_count = SEQ // BLOCK
    query_blocks = queries.reshape(block_count, BLOCK, QHEADS, HD)
    kv_blocks = keyvals.reshape(block_count, BLOCK, 2 * HD)
    before_blocks = jnp.concatenate([jnp.zeros_like(kv_blocks[:1]), kv_blocks[:-1]], 0)
    score_scale = HD ** (-0.5)

    def one_block(inputs):
        query_part, own_part, before_part, block_id = inputs
        key_rows = jnp.concatenate([own_part[:, :HD], before_part[:, :HD]], 0)
        value_rows = jnp.concatenate([own_part[:, HD:], before_part[:, HD:]], 0)
        scores = jnp.einsum('thd,kd->htk', query_part.astype(jnp.float32), key_rows.astype(jnp.float32)) * score_scale
        own_visible = block_pos[None, :] <= block_pos[:, None]
        before_visible = jnp.broadcast_to(block_id > 0, (BLOCK, BLOCK))
        visible = jnp.concatenate([own_visible, before_visible], 1)
        scores = jnp.where(visible[None], scores, -jnp.inf)
        top_score = lax.optimization_barrier(jnp.max(scores, axis=-1, keepdims=True))
        weights = jnp.where(visible[None], jnp.exp(scores - top_score), 0.0)
        totals = lax.optimization_barrier(jnp.sum(weights, axis=-1, keepdims=True))
        probs = weights.astype(jnp.bfloat16)
        mixed = jnp.einsum('htk,kd->htd', probs.astype(jnp.float32), value_rows.astype(jnp.float32)) / totals
        return mixed.transpose(1, 0, 2).reshape(BLOCK, QHEADS * HD).astype(jnp.bfloat16)
    attended = lax.map(one_block, (query_blocks, kv_blocks, before_blocks, jnp.arange(block_count, dtype=jnp.int32)))
    attended = attended.reshape(SEQ, QHEADS * HD)
    after_attn = (resid.astype(jnp.float32) + jnp.dot(attended, out_proj, preferred_element_type=jnp.float32)).astype(jnp.bfloat16)

    def mlp_block(rows_in):
        after_wide = rows_in.astype(jnp.float32)
        normed = (after_wide * lax.rsqrt(lax.optimization_barrier(jnp.mean(after_wide * after_wide, axis=-1, keepdims=True)) + 1e-05) * mlp_gain).astype(jnp.bfloat16)
        gate = jnp.dot(normed, w_gate, preferred_element_type=jnp.float32)
        upward = jnp.dot(normed, w_up, preferred_element_type=jnp.float32)
        hidden = (jax.nn.silu(gate) * upward).astype(jnp.bfloat16)
        mlp_sum = jnp.dot(hidden, w_down, preferred_element_type=jnp.float32)
        return (after_wide + mlp_sum).astype(jnp.bfloat16)
    layer_out = lax.map(mlp_block, after_attn.reshape(block_count, BLOCK, D))
    return layer_out.reshape(SEQ, D)
```

```python
import functools

import jax
import jax.numpy as jnp
from jax import lax
from jax.experimental import pallas as pl
from jax.experimental.pallas import tpu as pltpu
from jax.sharding import PartitionSpec as P

MESH = pl.DeviceIdType.MESH
F32 = jnp.float32
BF16 = jnp.bfloat16
EPS = 1e-05


def layer_kernel(
    n_out, n_in,
    order_ref, resid_ref, query_ref, kv_ref, proj_ref, gain_ref, wg_ref, wu_ref, wd_ref,
    out_ref,
    kv_all, wg, wu, wd, tok, after, hidden, x_out, x_in, own_part, z_out, z_in,
    kv_loc, kv_snd, kv_rcv, w_loc, w_pair_snd, w_snd, w_relay_snd, w_rcv,
    z_snd, z_rcv, x_snd, x_rcv, rx_snd, rx_rcv, rz_snd, rz_rcv,
):
    o = lax.axis_index("outer")
    i = lax.axis_index("inner")
    nz = n_out // 2
    z, x = o // 2, o % 2
    core = i % 2
    x_peer = (z * 2 + 1 - x, i)
    core_peer = (o, i + 1 - 2 * core)
    rows = resid_ref.shape[0]
    head = kv_ref.shape[1] // 2
    heads = query_ref.shape[1] // head
    pieces = order_ref.shape[0]
    block = n_in * rows
    span = block // pieces
    depth = wg_ref.shape[0]

    def remote(src, dst, ssem, rsem, device):
        return pltpu.make_async_remote_copy(
            src_ref=src, dst_ref=dst, send_sem=ssem, recv_sem=rsem,
            device_id=device, device_id_type=MESH,
        )

    barrier = pltpu.get_barrier_semaphore()
    after_o, before_o = lax.rem(o + 1, n_out), lax.rem(o + n_out - 1, n_out)
    count = 0
    for d in range(1, n_in):
        pl.semaphore_signal(barrier, inc=1, device_id=(o, lax.rem(i + d, n_in)), device_id_type=MESH)
        count += 1
    for d in range(n_in):
        for there in (after_o, before_o):
            pl.semaphore_signal(barrier, inc=1, device_id=(there, d), device_id_type=MESH)
            count += 1
    for d in range(1, nz):
        pl.semaphore_signal(
            barrier, inc=1, device_id=(lax.rem(z + d, nz) * 2 + x, i), device_id_type=MESH)
        count += 1
    pl.semaphore_signal(barrier, inc=1, device_id=x_peer, device_id_type=MESH)
    count += 1
    pl.semaphore_wait(barrier, count)

    own_rows = pl.ds(pl.multiple_of(i * rows, rows), rows)
    prev_rows = pl.ds(pl.multiple_of(block + i * rows, rows), rows)
    kv_copy = pltpu.make_async_copy(kv_ref, kv_all.at[own_rows], kv_loc)
    kv_copy.start()

    def kv_own(d):
        return remote(kv_ref, kv_all.at[own_rows], kv_snd.at[0, d], kv_rcv.at[0, d],
                      (o, lax.rem(i + d, n_in)))

    def kv_next(d):
        return remote(kv_ref, kv_all.at[prev_rows], kv_snd.at[1, d], kv_rcv.at[1, d],
                      (after_o, lax.rem(i + d, n_in)))

    for d in range(1, n_in):
        kv_own(d).start()

    @pl.when(o < n_out - 1)
    def _():
        for d in range(n_in):
            kv_next(d).start()

    def slot(k, q):
        if k == 2:
            return wd.at[q]
        full = wg if k == 0 else wu
        return full.at[pl.ds(pl.multiple_of(q * depth, depth), depth)]

    srcs = (wg_ref, wu_ref, wd_ref)
    steps = range(1, n_in // 2)

    def w_far(k, d):
        return remote(srcs[k], slot(k, i), w_snd.at[k, d], w_rcv.at[k, i],
                      (o, lax.rem(i + 2 * d, n_in)))

    def w_pair(k):
        return remote(srcs[k], slot(k, i), w_pair_snd.at[k], w_rcv.at[k, i], core_peer)

    def w_arrived(k, q):
        remote(slot(k, q), slot(k, q), w_pair_snd.at[k], w_rcv.at[k, q], core_peer).wait_recv()

    def w_relay(k, d):
        q = lax.rem(i + n_in - 2 * d, n_in)
        return remote(slot(k, q), slot(k, q), w_relay_snd.at[k, d], w_rcv.at[k, q], core_peer)

    def w_local(k):
        return pltpu.make_async_copy(srcs[k], slot(k, i), w_loc.at[k])

    for k in range(3):
        for d in steps:
            w_far(k, d).start()
    for k in range(3):
        w_pair(k).start()
        w_local(k).start()

    def relay_weight(k):
        for d in steps:
            w_arrived(k, lax.rem(i + n_in - 2 * d, n_in))
            w_relay(k, d).start()

    def weight_ready(k):
        w_local(k).wait()
        partner = i + 1 - 2 * core
        for d in range(n_in // 2):
            w_arrived(k, lax.rem(partner + 2 * d, n_in))

    lane = lax.broadcasted_iota(jnp.int32, (rows, block), 1)
    key_pos = jnp.zeros((rows, block), jnp.int32)
    for p in range(pieces):
        key_pos = jnp.where(lane // span == p, order_ref[p] * span + lane % span, key_pos)
    row = lax.broadcasted_iota(jnp.int32, (rows, block), 0)
    query_pos = jnp.zeros((rows, block), jnp.int32)
    for p in range(rows // span):
        query_pos = jnp.where(
            row // span == p, order_ref[i * (rows // span) + p] * span + row % span, query_pos)
    own_visible = key_pos <= query_pos
    before_visible = (jnp.zeros((rows, block), jnp.int32) + o) > 0

    @pl.when(o == 0)
    def _():
        kv_all[block:, :] = jnp.zeros((block, 2 * head), BF16)

    kv_copy.wait()
    for d in range(1, n_in):
        kv_own(d).wait_recv()

    @pl.when(o > 0)
    def _():
        for d in range(n_in):
            kv_next(d).wait_recv()

    parts = []
    nt = (((1,), (1,)), ((), ()))
    for h in range(heads):
        query = query_ref[:, h * head:(h + 1) * head]
        own_score = lax.dot_general(
            query, kv_all[:block, :head], nt, preferred_element_type=F32) * head ** (-0.5)
        before_score = lax.dot_general(
            query, kv_all[block:, :head], nt, preferred_element_type=F32) * head ** (-0.5)
        own_score = jnp.where(own_visible, own_score, -1e30)
        before_score = jnp.where(before_visible, before_score, -1e30)
        top = jnp.maximum(
            jnp.max(own_score, axis=1, keepdims=True), jnp.max(before_score, axis=1, keepdims=True))
        own_w = jnp.where(own_visible, jnp.exp(own_score - top), 0.0)
        before_w = jnp.where(before_visible, jnp.exp(before_score - top), 0.0)
        total = jnp.sum(own_w, axis=1, keepdims=True) + jnp.sum(before_w, axis=1, keepdims=True)
        mixed = jnp.dot(own_w.astype(BF16), kv_all[:block, head:], preferred_element_type=F32)
        mixed += jnp.dot(before_w.astype(BF16), kv_all[block:, head:], preferred_element_type=F32)
        parts.append((mixed / total).astype(BF16))
    attended = jnp.concatenate(parts, axis=1)
    after_attn = (
        resid_ref[...].astype(F32) + jnp.dot(attended, proj_ref[...], preferred_element_type=F32)
    ).astype(BF16)
    after[...] = after_attn
    wide = after_attn.astype(F32)
    normed = wide * lax.rsqrt(jnp.mean(wide * wide, axis=1, keepdims=True) + EPS) * gain_ref[...]

    def tok_rows(zz, xx):
        return tok.at[pl.ds(pl.multiple_of((zz * 2 + xx) * rows, rows), rows)]

    tok_rows(z, x)[...] = normed.astype(BF16)

    def tok_z(d):
        return remote(tok_rows(z, x), tok_rows(z, x), z_snd.at[d], z_rcv.at[d],
                      (lax.rem(z + d, nz) * 2 + x, i))

    def tok_z_arrived(d):
        here = tok_rows(lax.rem(z + nz - d, nz), x)
        remote(here, here, z_snd.at[d], z_rcv.at[d], x_peer).wait_recv()

    def tok_x(d):
        here = tok_rows(lax.rem(z + nz - d, nz), x)
        return remote(here, here, x_snd.at[d], x_rcv.at[d], x_peer)

    def tok_x_arrived(d):
        here = tok_rows(lax.rem(z + nz - d, nz), 1 - x)
        remote(here, here, x_snd.at[d], x_rcv.at[d], x_peer).wait_recv()

    tok_x(0).start()
    for d in range(1, nz):
        tok_z(d).start()
    relayed = 0
    for d in range(1, nz):
        tok_z_arrived(d)
        tok_x(d).start()
        if d < nz - 1 and relayed < 2:
            relay_weight(relayed)
            relayed += 1
    for k in range(relayed, 2):
        relay_weight(k)
    weight_ready(0)
    weight_ready(1)

    def pair_rows(zz):
        return pl.ds(pl.multiple_of(zz * 2 * rows, 2 * rows), 2 * rows)

    def hidden_step(d, carry):
        tok_x_arrived(d)
        here = pair_rows(lax.rem(z + nz - d, nz))
        tokens = tok[here, :]
        gate = jnp.dot(tokens, wg[...], preferred_element_type=F32)
        upward = jnp.dot(tokens, wu[...], preferred_element_type=F32)
        hidden[here, :] = (gate / (1.0 + jnp.exp(-gate)) * upward).astype(BF16)
        return carry

    lax.fori_loop(0, nz, hidden_step, 0)
    relay_weight(2)
    weight_ready(2)

    def sum_x(t):
        return remote(x_out.at[t], x_in.at[t], rx_snd.at[t], rx_rcv.at[t], x_peer)

    def sum_z(t):
        return remote(z_out.at[t], z_in.at[t], rz_snd.at[t], rz_rcv.at[t],
                      (lax.rem(z + 1 + t, nz) * 2 + x, i))

    width = wd_ref.shape[1]

    def finish(t):
        sum_x(t).wait_recv()
        z_out[t] = (own_part[t] + x_in[t].astype(F32)).astype(BF16)
        sum_z(t).start()

    def down_step(t, carry):
        zz = lax.rem(z + 1 + t, nz)

        def half(xx):
            return hidden[pl.ds(pl.multiple_of((zz * 2 + xx) * rows, rows), rows), :]

        both = jnp.concatenate([half(1 - x), half(x)], axis=0)
        for q in range(n_in):
            part = jnp.dot(both, wd[q], preferred_element_type=F32)
            x_out[t, :, q * width:(q + 1) * width] = part[:rows].astype(BF16)
            own_part[t, :, q * width:(q + 1) * width] = part[rows:]
        sum_x(t).start()

        @pl.when(t >= 1)
        def _():
            finish(t - 1)

        return carry

    lax.fori_loop(0, nz, down_step, 0)
    last = nz - 1
    sum_x(last).wait_recv()
    result = after[...].astype(F32) + own_part[last] + x_in[last].astype(F32)
    for t in range(last):
        sum_z(t).wait_recv()
        result += z_in[t].astype(F32)
    out_ref[...] = result.astype(BF16)

    for d in range(1, n_in):
        kv_own(d).wait_send()

    @pl.when(o < n_out - 1)
    def _():
        for d in range(n_in):
            kv_next(d).wait_send()

    for k in range(3):
        w_pair(k).wait_send()
        for d in steps:
            w_far(k, d).wait_send()
            w_relay(k, d).wait_send()
    for d in range(1, nz):
        tok_z(d).wait_send()
    for d in range(nz):
        tok_x(d).wait_send()
        sum_x(d).wait_send()
    for t in range(last):
        sum_z(t).wait_send()


def per_device(n_out, n_in, resid, queries, keyvals, piece_order, out_proj, mlp_gain, w_gate, w_up, w_down):
    rows, model = resid.shape
    units = w_gate.shape[1]
    nz = n_out // 2
    dma = pltpu.SemaphoreType.DMA
    vmem = pl.BlockSpec(memory_space=pltpu.VMEM)
    hbm = pl.BlockSpec(memory_space=pl.ANY)
    return pl.pallas_call(
        functools.partial(layer_kernel, n_out, n_in),
        out_shape=jax.ShapeDtypeStruct(resid.shape, BF16),
        in_specs=[pl.BlockSpec(memory_space=pltpu.SMEM)] + [vmem] * 5 + [hbm] * 3,
        out_specs=vmem,
        scratch_shapes=[
            pltpu.VMEM((2 * n_in * rows, keyvals.shape[1]), BF16),
            pltpu.VMEM((model, units), BF16),
            pltpu.VMEM((model, units), BF16),
            pltpu.VMEM((n_in,) + w_down.shape, BF16),
            pltpu.VMEM((n_out * rows, model), BF16),
            pltpu.VMEM((rows, model), BF16),
            pltpu.VMEM((n_out * rows, units), BF16),
            pltpu.VMEM((nz, rows, model), BF16),
            pltpu.VMEM((nz, rows, model), BF16),
            pltpu.VMEM((nz, rows, model), F32),
            pltpu.VMEM((nz - 1, rows, model), BF16),
            pltpu.VMEM((nz - 1, rows, model), BF16),
            dma(()), dma((2, n_in)), dma((2, n_in)),
            dma((3,)), dma((3,)), dma((3, n_in)), dma((3, n_in)), dma((3, n_in)),
            dma((nz,)), dma((nz,)), dma((nz,)), dma((nz,)),
            dma((nz,)), dma((nz,)), dma((nz,)), dma((nz,)),
        ],
        compiler_params=pltpu.CompilerParams(
            collective_id=0, has_side_effects=True, vmem_limit_bytes=60000 * 1024
        ),
        name="layer",
    )(piece_order, resid, queries, keyvals, out_proj, mlp_gain.reshape(1, -1), w_gate, w_up, w_down)


def solution(mesh):
    placed = (
        P(("outer", "inner"), None),
        P(("outer", "inner"), None),
        P(("outer", "inner"), None),
        P(),
        P(),
        P(),
        P("inner", "outer"),
        P("inner", "outer"),
        P("outer", "inner"),
    )
    return jax.shard_map(
        functools.partial(per_device, mesh.shape["outer"], mesh.shape["inner"]),
        mesh=mesh,
        in_specs=placed,
        out_specs=P(("outer", "inner"), None),
        check_vma=False,
    )
```

```python
import functools

import jax
import jax.numpy as jnp
from jax import lax
from jax.experimental import pallas as pl
from jax.experimental.pallas import tpu as pltpu
from jax.sharding import PartitionSpec as P

MESH = pl.DeviceIdType.MESH
F32 = jnp.float32
BF16 = jnp.bfloat16
EPS = 1e-05


def layer_kernel(
    n_out, n_in,
    order_ref, resid_ref, query_ref, kv_ref, proj_ref, gain_ref, wg_ref, wu_ref, wd_ref,
    out_ref,
    kv_all, wg, wu, wd, tok, after, hidden, x_out, x_in, own_part, z_out, z_in,
    kv_loc, kv_snd, kv_rcv, w_loc, w_pair_snd, w_snd, w_relay_snd, w_rcv,
    z_snd, z_rcv, x_snd, x_rcv, rx_snd, rx_rcv, rz_snd, rz_rcv,
):
    o = lax.axis_index("outer")
    i = lax.axis_index("inner")
    nz = n_out // 2
    z, x = o // 2, o % 2
    core = i % 2
    x_peer = (z * 2 + 1 - x, i)
    core_peer = (o, i + 1 - 2 * core)
    rows = resid_ref.shape[0]
    head = kv_ref.shape[1] // 2
    heads = query_ref.shape[1] // head
    pieces = order_ref.shape[0]
    block = n_in * rows
    span = block // pieces
    depth = wg_ref.shape[0]

    def remote(src, dst, ssem, rsem, device):
        return pltpu.make_async_remote_copy(
            src_ref=src, dst_ref=dst, send_sem=ssem, recv_sem=rsem,
            device_id=device, device_id_type=MESH,
        )

    barrier = pltpu.get_barrier_semaphore()
    after_o, before_o = lax.rem(o + 1, n_out), lax.rem(o + n_out - 1, n_out)
    count = 0
    for d in range(1, n_in):
        pl.semaphore_signal(barrier, inc=1, device_id=(o, lax.rem(i + d, n_in)), device_id_type=MESH)
        count += 1
    for d in range(n_in):
        for there in (after_o, before_o):
            pl.semaphore_signal(barrier, inc=1, device_id=(there, d), device_id_type=MESH)
            count += 1
    for d in range(1, nz):
        pl.semaphore_signal(
            barrier, inc=1, device_id=(lax.rem(z + d, nz) * 2 + x, i), device_id_type=MESH)
        count += 1
    pl.semaphore_signal(barrier, inc=1, device_id=x_peer, device_id_type=MESH)
    count += 1
    pl.semaphore_wait(barrier, count)

    own_rows = pl.ds(pl.multiple_of(i * rows, rows), rows)
    prev_rows = pl.ds(pl.multiple_of(block + i * rows, rows), rows)
    kv_copy = pltpu.make_async_copy(kv_ref, kv_all.at[own_rows], kv_loc)
    kv_copy.start()

    def kv_own(d):
        return remote(kv_ref, kv_all.at[own_rows], kv_snd.at[0, d], kv_rcv.at[0, d],
                      (o, lax.rem(i + d, n_in)))

    def kv_next(d):
        return remote(kv_ref, kv_all.at[prev_rows], kv_snd.at[1, d], kv_rcv.at[1, d],
                      (after_o, lax.rem(i + d, n_in)))

    for d in range(1, n_in):
        kv_own(d).start()

    @pl.when(o < n_out - 1)
    def _():
        for d in range(n_in):
            kv_next(d).start()

    def slot(k, q):
        if k == 2:
            return wd.at[q]
        full = wg if k == 0 else wu
        return full.at[pl.ds(pl.multiple_of(q * depth, depth), depth)]

    srcs = (wg_ref, wu_ref, wd_ref)
    steps = range(1, n_in // 2)

    def w_far(k, d):
        return remote(srcs[k], slot(k, i), w_snd.at[k, d], w_rcv.at[k, i],
                      (o, lax.rem(i + 2 * d, n_in)))

    def w_pair(k):
        return remote(srcs[k], slot(k, i), w_pair_snd.at[k], w_rcv.at[k, i], core_peer)

    def w_arrived(k, q):
        remote(slot(k, q), slot(k, q), w_pair_snd.at[k], w_rcv.at[k, q], core_peer).wait_recv()

    def w_relay(k, d):
        q = lax.rem(i + n_in - 2 * d, n_in)
        return remote(slot(k, q), slot(k, q), w_relay_snd.at[k, d], w_rcv.at[k, q], core_peer)

    def w_local(k):
        return pltpu.make_async_copy(srcs[k], slot(k, i), w_loc.at[k])

    for k in range(3):
        for d in steps:
            w_far(k, d).start()
    for k in range(3):
        w_pair(k).start()
        w_local(k).start()

    def relay_weight(k):
        for d in steps:
            w_arrived(k, lax.rem(i + n_in - 2 * d, n_in))
            w_relay(k, d).start()

    def weight_ready(k):
        w_local(k).wait()
        partner = i + 1 - 2 * core
        for d in range(n_in // 2):
            w_arrived(k, lax.rem(partner + 2 * d, n_in))

    lane = lax.broadcasted_iota(jnp.int32, (rows, block), 1)
    key_pos = jnp.zeros((rows, block), jnp.int32)
    for p in range(pieces):
        key_pos = jnp.where(lane // span == p, order_ref[p] * span + lane % span, key_pos)
    row = lax.broadcasted_iota(jnp.int32, (rows, block), 0)
    query_pos = jnp.zeros((rows, block), jnp.int32)
    for p in range(rows // span):
        query_pos = jnp.where(
            row // span == p, order_ref[i * (rows // span) + p] * span + row % span, query_pos)
    own_visible = key_pos <= query_pos
    before_visible = (jnp.zeros((rows, block), jnp.int32) + o) > 0

    @pl.when(o == 0)
    def _():
        kv_all[block:, :] = jnp.zeros((block, 2 * head), BF16)

    kv_copy.wait()
    for d in range(1, n_in):
        kv_own(d).wait_recv()

    @pl.when(o > 0)
    def _():
        for d in range(n_in):
            kv_next(d).wait_recv()

    parts = []
    nt = (((1,), (1,)), ((), ()))
    for h in range(heads):
        query = query_ref[:, h * head:(h + 1) * head]
        own_score = lax.dot_general(
            query, kv_all[:block, :head], nt, preferred_element_type=F32) * head ** (-0.5)
        before_score = lax.dot_general(
            query, kv_all[block:, :head], nt, preferred_element_type=F32) * head ** (-0.5)
        own_score = jnp.where(own_visible, own_score, -1e30)
        before_score = jnp.where(before_visible, before_score, -1e30)
        top = jnp.maximum(
            jnp.max(own_score, axis=1, keepdims=True), jnp.max(before_score, axis=1, keepdims=True))
        own_w = jnp.where(own_visible, jnp.exp(own_score - top), 0.0)
        before_w = jnp.where(before_visible, jnp.exp(before_score - top), 0.0)
        total = jnp.sum(own_w, axis=1, keepdims=True) + jnp.sum(before_w, axis=1, keepdims=True)
        mixed = jnp.dot(own_w.astype(BF16), kv_all[:block, head:], preferred_element_type=F32)
        mixed += jnp.dot(before_w.astype(BF16), kv_all[block:, head:], preferred_element_type=F32)
        parts.append((mixed / total).astype(BF16))
    attended = jnp.concatenate(parts, axis=1)
    after_attn = (
        resid_ref[...].astype(F32) + jnp.dot(attended, proj_ref[...], preferred_element_type=F32)
    ).astype(BF16)
    after[...] = after_attn
    wide = after_attn.astype(F32)
    normed = wide * lax.rsqrt(jnp.mean(wide * wide, axis=1, keepdims=True) + EPS) * gain_ref[...]

    def tok_rows(zz, xx):
        return tok.at[pl.ds(pl.multiple_of((zz * 2 + xx) * rows, rows), rows)]

    tok_rows(z, x)[...] = normed.astype(BF16)

    def z_device(zz):
        return (zz * 2 + x, i)

    def inside(zz):
        return jnp.logical_and(zz >= 0, zz < nz)

    def tok_z(way, h):
        step = 1 - 2 * way
        here = tok_rows(z - step * h, x)
        return remote(here, here, z_snd.at[way, h], z_rcv.at[way, h], z_device(z + step))

    def tok_z_arrived(way, h):
        here = tok_rows(z - (1 - 2 * way) * (h + 1), x)
        remote(here, here, z_snd.at[way, h], z_rcv.at[way, h], x_peer).wait_recv()

    def tok_x(zz):
        here = tok_rows(zz, x)
        return remote(here, here, x_snd.at[zz], x_rcv.at[zz], x_peer)

    def tok_x_arrived(zz):
        here = tok_rows(zz, 1 - x)
        remote(here, here, x_snd.at[zz], x_rcv.at[zz], x_peer).wait_recv()

    for way in range(2):
        @pl.when(inside(z + 1 - 2 * way))
        def _():
            tok_z(way, 0).start()
    tok_x(z).start()
    for h in range(nz - 1):
        for way in range(2):
            step = 1 - 2 * way
            source = z - step * (h + 1)

            @pl.when(inside(source))
            def _():
                tok_z_arrived(way, h)

                @pl.when(inside(z + step))
                def _():
                    tok_z(way, h + 1).start()

                tok_x(source).start()
        if h < 2:
            relay_weight(h)
    for k in range(min(nz - 1, 2), 2):
        relay_weight(k)
    weight_ready(0)
    weight_ready(1)

    def hidden_step(j, carry):
        zz = z + ((j + 1) // 2) * (1 - 2 * (j % 2))

        @pl.when(inside(zz))
        def _():
            tok_x_arrived(zz)
            here = pl.ds(pl.multiple_of(zz * 2 * rows, 2 * rows), 2 * rows)
            tokens = tok[here, :]
            gate = jnp.dot(tokens, wg[...], preferred_element_type=F32)
            upward = jnp.dot(tokens, wu[...], preferred_element_type=F32)
            hidden[here, :] = (gate / (1.0 + jnp.exp(-gate)) * upward).astype(BF16)

        return carry

    lax.fori_loop(0, 2 * nz - 1, hidden_step, 0)
    relay_weight(2)
    weight_ready(2)

    def sum_x(zz):
        return remote(x_out.at[zz], x_in.at[zz], rx_snd.at[zz], rx_rcv.at[zz], x_peer)

    def sum_z(way, zz):
        step = jnp.where(inside(z + 1 - 2 * way), 1 - 2 * way, 0)
        return remote(z_out.at[zz], z_in.at[way, zz], rz_snd.at[zz], rz_rcv.at[way, zz],
                      z_device(z + step))

    width = wd_ref.shape[1]

    def owner(j):
        way = j % 2
        return way, z + (nz - 1 - j // 2) * (1 - 2 * way)

    def down_step(j, carry):
        way, zz = owner(j)

        @pl.when(inside(zz))
        def _():
            def half(xx):
                return hidden[pl.ds(pl.multiple_of((zz * 2 + xx) * rows, rows), rows), :]

            both = jnp.concatenate([half(1 - x), half(x)], axis=0)
            for q in range(n_in):
                part = jnp.dot(both, wd[q], preferred_element_type=F32)
                x_out[zz, :, q * width:(q + 1) * width] = part[:rows].astype(BF16)
                own_part[zz, :, q * width:(q + 1) * width] = part[rows:]
            sum_x(zz).start()

        return carry

    lax.fori_loop(0, 2 * nz - 1, down_step, 0)

    def finish_step(j, carry):
        way, zz = owner(j)
        more = inside(z - (1 - 2 * way))

        @pl.when(inside(zz))
        def _():
            sum_x(zz).wait_recv()

            @pl.when(more)
            def _():
                sum_z(way, zz).wait_recv()
                z_out[zz] = (
                    own_part[zz] + x_in[zz].astype(F32) + z_in[way, zz].astype(F32)).astype(BF16)

            @pl.when(jnp.logical_not(more))
            def _():
                z_out[zz] = (own_part[zz] + x_in[zz].astype(F32)).astype(BF16)

            sum_z(way, zz).start()

        return carry

    lax.fori_loop(0, 2 * nz - 2, finish_step, 0)
    for way in range(2):
        @pl.when(inside(z - (1 - 2 * way)))
        def _():
            sum_z(way, z).wait_recv()
            own_part[z] = own_part[z] + z_in[way, z].astype(F32)
    sum_x(z).wait_recv()
    out_ref[...] = (after[...].astype(F32) + (own_part[z] + x_in[z].astype(F32))).astype(BF16)

    for d in range(1, n_in):
        kv_own(d).wait_send()

    @pl.when(o < n_out - 1)
    def _():
        for d in range(n_in):
            kv_next(d).wait_send()

    for k in range(3):
        w_pair(k).wait_send()
        for d in steps:
            w_far(k, d).wait_send()
            w_relay(k, d).wait_send()
    for h in range(nz - 1):
        for way in range(2):
            step = 1 - 2 * way

            @pl.when(jnp.logical_and(inside(z - step * h), inside(z + step)))
            def _():
                tok_z(way, h).wait_send()
    for zz in range(nz):
        tok_x(zz).wait_send()
        sum_x(zz).wait_send()

        @pl.when(z != zz)
        def _():
            sum_z(0, zz).wait_send()


def per_device(n_out, n_in, resid, queries, keyvals, piece_order, out_proj, mlp_gain, w_gate, w_up, w_down):
    rows, model = resid.shape
    units = w_gate.shape[1]
    nz = n_out // 2
    dma = pltpu.SemaphoreType.DMA
    vmem = pl.BlockSpec(memory_space=pltpu.VMEM)
    hbm = pl.BlockSpec(memory_space=pl.ANY)
    return pl.pallas_call(
        functools.partial(layer_kernel, n_out, n_in),
        out_shape=jax.ShapeDtypeStruct(resid.shape, BF16),
        in_specs=[pl.BlockSpec(memory_space=pltpu.SMEM)] + [vmem] * 5 + [hbm] * 3,
        out_specs=vmem,
        scratch_shapes=[
            pltpu.VMEM((2 * n_in * rows, keyvals.shape[1]), BF16),
            pltpu.VMEM((model, units), BF16),
            pltpu.VMEM((model, units), BF16),
            pltpu.VMEM((n_in,) + w_down.shape, BF16),
            pltpu.VMEM((n_out * rows, model), BF16),
            pltpu.VMEM((rows, model), BF16),
            pltpu.VMEM((n_out * rows, units), BF16),
            pltpu.VMEM((nz, rows, model), BF16),
            pltpu.VMEM((nz, rows, model), BF16),
            pltpu.VMEM((nz, rows, model), F32),
            pltpu.VMEM((nz, rows, model), BF16),
            pltpu.VMEM((2, nz, rows, model), BF16),
            dma(()), dma((2, n_in)), dma((2, n_in)),
            dma((3,)), dma((3,)), dma((3, n_in)), dma((3, n_in)), dma((3, n_in)),
            dma((2, nz)), dma((2, nz)), dma((nz,)), dma((nz,)),
            dma((nz,)), dma((nz,)), dma((nz,)), dma((2, nz)),
        ],
        compiler_params=pltpu.CompilerParams(
            collective_id=0, has_side_effects=True, vmem_limit_bytes=60000 * 1024
        ),
        name="layer",
    )(piece_order, resid, queries, keyvals, out_proj, mlp_gain.reshape(1, -1), w_gate, w_up, w_down)


def solution(mesh):
    placed = (
        P(("outer", "inner"), None),
        P(("outer", "inner"), None),
        P(("outer", "inner"), None),
        P(),
        P(),
        P(),
        P("inner", "outer"),
        P("inner", "outer"),
        P("outer", "inner"),
    )
    return jax.shard_map(
        functools.partial(per_device, mesh.shape["outer"], mesh.shape["inner"]),
        mesh=mesh,
        in_specs=placed,
        out_specs=P(("outer", "inner"), None),
        check_vma=False,
    )
```

```python
import functools

import jax
import jax.numpy as jnp
from jax import lax
from jax.experimental import pallas as pl
from jax.experimental.pallas import tpu as pltpu
from jax.sharding import PartitionSpec as P

MESH = pl.DeviceIdType.MESH
F32 = jnp.float32
BF16 = jnp.bfloat16
EPS = 1e-05


def layer_kernel(
    n_out, n_in,
    order_ref, resid_ref, query_ref, kv_ref, proj_ref, gain_ref, wg_ref, wu_ref, wd_ref,
    out_ref,
    kv_all, wg, wu, wd, tok, after, hidden, x_out, x_in, own_part, z_out, z_in,
    kv_loc, kv_nxt_snd, kv_snd, kv_rcv, w_loc, w_pair_snd, w_snd, w_relay_snd, w_rcv,
    z_snd, z_rcv, x_snd, x_rcv, rx_snd, rx_rcv, rz_snd, rz_rcv,
):
    o = lax.axis_index("outer")
    i = lax.axis_index("inner")
    nz = n_out // 2
    z, x = o // 2, o % 2
    core = i % 2
    x_peer = (z * 2 + 1 - x, i)
    core_peer = (o, i + 1 - 2 * core)
    rows = resid_ref.shape[0]
    head = kv_ref.shape[1] // 2
    heads = query_ref.shape[1] // head
    pieces = order_ref.shape[0]
    block = n_in * rows
    span = block // pieces
    depth = wg_ref.shape[0]

    def remote(src, dst, ssem, rsem, device):
        return pltpu.make_async_remote_copy(
            src_ref=src, dst_ref=dst, send_sem=ssem, recv_sem=rsem,
            device_id=device, device_id_type=MESH,
        )

    barrier = pltpu.get_barrier_semaphore()
    after_o, before_o = lax.rem(o + 1, n_out), lax.rem(o + n_out - 1, n_out)
    count = 0
    for d in range(1, n_in):
        pl.semaphore_signal(barrier, inc=1, device_id=(o, lax.rem(i + d, n_in)), device_id_type=MESH)
        count += 1
    for there in (after_o, before_o):
        pl.semaphore_signal(barrier, inc=1, device_id=(there, i), device_id_type=MESH)
        count += 1
    for d in range(1, nz):
        pl.semaphore_signal(
            barrier, inc=1, device_id=(lax.rem(z + d, nz) * 2 + x, i), device_id_type=MESH)
        count += 1
    pl.semaphore_signal(barrier, inc=1, device_id=x_peer, device_id_type=MESH)
    count += 1
    pl.semaphore_wait(barrier, count)

    own_rows = pl.ds(pl.multiple_of(i * rows, rows), rows)
    kv_copy = pltpu.make_async_copy(kv_ref, kv_all.at[own_rows], kv_loc)
    kv_copy.start()

    steps = range(1, n_in // 2)

    def kv_slot(part, q):
        return kv_all.at[pl.ds(pl.multiple_of(part * block + q * rows, rows), rows)]

    def kv_send(part, d):
        to = core_peer if d == 0 else (o, lax.rem(i + 2 * d, n_in))
        src = kv_ref if part == 0 else kv_slot(1, i)
        return remote(src, kv_slot(part, i), kv_snd.at[part, d], kv_rcv.at[part, i], to)

    def kv_relay(part, d):
        here = kv_slot(part, lax.rem(i + n_in - 2 * d, n_in))
        return remote(here, here, kv_snd.at[part, n_in // 2 + d],
                      kv_rcv.at[part, lax.rem(i + n_in - 2 * d, n_in)], core_peer)

    def kv_arrived(part, q):
        remote(kv_slot(part, q), kv_slot(part, q), kv_snd.at[part, 0], kv_rcv.at[part, q], core_peer).wait_recv()

    def kv_next():
        return remote(kv_ref, kv_slot(1, i), kv_nxt_snd, kv_rcv.at[1, i], (after_o, i))

    @pl.when(o < n_out - 1)
    def _():
        kv_next().start()

    for d in range(n_in // 2):
        kv_send(0, d).start()

    def slot(k, q):
        if k == 2:
            return wd.at[q]
        full = wg if k == 0 else wu
        return full.at[pl.ds(pl.multiple_of(q * depth, depth), depth)]

    srcs = (wg_ref, wu_ref, wd_ref)
    def w_far(k, d):
        return remote(srcs[k], slot(k, i), w_snd.at[k, d], w_rcv.at[k, i],
                      (o, lax.rem(i + 2 * d, n_in)))

    def w_pair(k):
        return remote(srcs[k], slot(k, i), w_pair_snd.at[k], w_rcv.at[k, i], core_peer)

    def w_arrived(k, q):
        remote(slot(k, q), slot(k, q), w_pair_snd.at[k], w_rcv.at[k, q], core_peer).wait_recv()

    def w_relay(k, d):
        q = lax.rem(i + n_in - 2 * d, n_in)
        return remote(slot(k, q), slot(k, q), w_relay_snd.at[k, d], w_rcv.at[k, q], core_peer)

    def w_local(k):
        return pltpu.make_async_copy(srcs[k], slot(k, i), w_loc.at[k])

    for k in range(3):
        for d in steps:
            w_far(k, d).start()
    for k in range(3):
        w_pair(k).start()
        w_local(k).start()

    def relay_weight(k):
        for d in steps:
            w_arrived(k, lax.rem(i + n_in - 2 * d, n_in))
            w_relay(k, d).start()

    def weight_ready(k):
        w_local(k).wait()
        for d in range(n_in // 2):
            w_arrived(k, lax.rem(partner + 2 * d, n_in))

    lane = lax.broadcasted_iota(jnp.int32, (rows, block), 1)
    key_pos = jnp.zeros((rows, block), jnp.int32)
    for p in range(pieces):
        key_pos = jnp.where(lane // span == p, order_ref[p] * span + lane % span, key_pos)
    row = lax.broadcasted_iota(jnp.int32, (rows, block), 0)
    query_pos = jnp.zeros((rows, block), jnp.int32)
    for p in range(rows // span):
        query_pos = jnp.where(
            row // span == p, order_ref[i * (rows // span) + p] * span + row % span, query_pos)
    own_visible = key_pos <= query_pos
    before_visible = (jnp.zeros((rows, block), jnp.int32) + o) > 0

    @pl.when(o == 0)
    def _():
        kv_all[block:, :] = jnp.zeros((block, 2 * head), BF16)

    @pl.when(o > 0)
    def _():
        kv_arrived(1, i)
        for d in range(n_in // 2):
            kv_send(1, d).start()

    for d in steps:
        kv_arrived(0, lax.rem(i + n_in - 2 * d, n_in))
        kv_relay(0, d).start()

    @pl.when(o > 0)
    def _():
        for d in steps:
            kv_arrived(1, lax.rem(i + n_in - 2 * d, n_in))
            kv_relay(1, d).start()

    partner = i + 1 - 2 * core
    kv_copy.wait()
    for d in range(n_in // 2):
        kv_arrived(0, lax.rem(partner + 2 * d, n_in))

    @pl.when(o > 0)
    def _():
        for d in range(n_in // 2):
            kv_arrived(1, lax.rem(partner + 2 * d, n_in))

    parts = []
    nt = (((1,), (1,)), ((), ()))
    for h in range(heads):
        query = query_ref[:, h * head:(h + 1) * head]
        own_score = lax.dot_general(
            query, kv_all[:block, :head], nt, preferred_element_type=F32) * head ** (-0.5)
        before_score = lax.dot_general(
            query, kv_all[block:, :head], nt, preferred_element_type=F32) * head ** (-0.5)
        own_score = jnp.where(own_visible, own_score, -1e30)
        before_score = jnp.where(before_visible, before_score, -1e30)
        top = jnp.maximum(
            jnp.max(own_score, axis=1, keepdims=True), jnp.max(before_score, axis=1, keepdims=True))
        own_w = jnp.where(own_visible, jnp.exp(own_score - top), 0.0)
        before_w = jnp.where(before_visible, jnp.exp(before_score - top), 0.0)
        total = jnp.sum(own_w, axis=1, keepdims=True) + jnp.sum(before_w, axis=1, keepdims=True)
        mixed = jnp.dot(own_w.astype(BF16), kv_all[:block, head:], preferred_element_type=F32)
        mixed += jnp.dot(before_w.astype(BF16), kv_all[block:, head:], preferred_element_type=F32)
        parts.append((mixed / total).astype(BF16))
    attended = jnp.concatenate(parts, axis=1)
    after_attn = (
        resid_ref[...].astype(F32) + jnp.dot(attended, proj_ref[...], preferred_element_type=F32)
    ).astype(BF16)
    after[...] = after_attn
    wide = after_attn.astype(F32)
    normed = wide * lax.rsqrt(jnp.mean(wide * wide, axis=1, keepdims=True) + EPS) * gain_ref[...]

    def tok_rows(zz, xx):
        return tok.at[pl.ds(pl.multiple_of((zz * 2 + xx) * rows, rows), rows)]

    tok_rows(z, x)[...] = normed.astype(BF16)

    def z_device(zz):
        return (zz * 2 + x, i)

    def inside(zz):
        return jnp.logical_and(zz >= 0, zz < nz)

    def tok_z(way, h):
        step = 1 - 2 * way
        here = tok_rows(z - step * h, x)
        return remote(here, here, z_snd.at[way, h], z_rcv.at[way, h], z_device(z + step))

    def tok_z_arrived(way, h):
        here = tok_rows(z - (1 - 2 * way) * (h + 1), x)
        remote(here, here, z_snd.at[way, h], z_rcv.at[way, h], x_peer).wait_recv()

    def tok_x(zz):
        here = tok_rows(zz, x)
        return remote(here, here, x_snd.at[zz], x_rcv.at[zz], x_peer)

    def tok_x_arrived(zz):
        here = tok_rows(zz, 1 - x)
        remote(here, here, x_snd.at[zz], x_rcv.at[zz], x_peer).wait_recv()

    for way in range(2):
        @pl.when(inside(z + 1 - 2 * way))
        def _():
            tok_z(way, 0).start()
    tok_x(z).start()
    for h in range(nz - 1):
        for way in range(2):
            step = 1 - 2 * way
            source = z - step * (h + 1)

            @pl.when(inside(source))
            def _():
                tok_z_arrived(way, h)

                @pl.when(inside(z + step))
                def _():
                    tok_z(way, h + 1).start()

                tok_x(source).start()
        if h < 2:
            relay_weight(h)
    for k in range(min(nz - 1, 2), 2):
        relay_weight(k)
    weight_ready(0)
    weight_ready(1)

    chunks = n_in // 2
    width = wd_ref.shape[1]

    def columns_of(p):
        return lax.rem(i // 2 + chunks - p, chunks)

    def sum_x(p, zz):
        return remote(x_out.at[p, zz], x_in.at[p, zz], rx_snd.at[p, zz], rx_rcv.at[p, zz], x_peer)

    def sum_z(p, way, zz):
        step = jnp.where(inside(z + 1 - 2 * way), 1 - 2 * way, 0)
        return remote(z_out.at[p, zz], z_in.at[p, way, zz], rz_snd.at[p, zz], rz_rcv.at[p, way, zz],
                      z_device(z + step))

    def down(p, zz):
        def half(xx):
            return hidden[pl.ds(pl.multiple_of((zz * 2 + xx) * rows, rows), rows), :]

        both = jnp.concatenate([half(1 - x), half(x)], axis=0)
        for q in range(2):
            part = jnp.dot(both, wd[2 * columns_of(p) + q], preferred_element_type=F32)
            x_out[p, zz, :, q * width:(q + 1) * width] = part[:rows].astype(BF16)
            own_part[p, zz, :, q * width:(q + 1) * width] = part[rows:]
        sum_x(p, zz).start()

    def owner(j):
        way = j % 2
        return way, z + (nz - 1 - j // 2) * (1 - 2 * way)

    def finish(p, j):
        way, zz = owner(j)
        more = inside(z - (1 - 2 * way))

        @pl.when(inside(zz))
        def _():
            sum_x(p, zz).wait_recv()

            @pl.when(more)
            def _():
                sum_z(p, way, zz).wait_recv()
                z_out[p, zz] = (
                    own_part[p, zz] + x_in[p, zz].astype(F32) + z_in[p, way, zz].astype(F32)
                ).astype(BF16)

            @pl.when(jnp.logical_not(more))
            def _():
                z_out[p, zz] = (own_part[p, zz] + x_in[p, zz].astype(F32)).astype(BF16)

            sum_z(p, way, zz).start()

    w_local(2).wait()
    w_arrived(2, partner)

    def hidden_step(j, carry):
        zz = z + ((j + 1) // 2) * (1 - 2 * (j % 2))

        @pl.when(inside(zz))
        def _():
            tok_x_arrived(zz)
            here = pl.ds(pl.multiple_of(zz * 2 * rows, 2 * rows), 2 * rows)
            tokens = tok[here, :]
            gate = jnp.dot(tokens, wg[...], preferred_element_type=F32)
            upward = jnp.dot(tokens, wu[...], preferred_element_type=F32)
            hidden[here, :] = (gate / (1.0 + jnp.exp(-gate)) * upward).astype(BF16)

            @pl.when(j < 3)
            def _():
                down(0, zz)

        return carry

    lax.fori_loop(0, 2 * nz - 1, hidden_step, 0)

    def down_first(j, carry):
        _, zz = owner(j)

        @pl.when(inside(zz))
        def _():
            down(0, zz)

        return carry

    lax.fori_loop(0, 2 * (nz - 2), down_first, 0)
    relay_weight(2)
    for d in range(1, n_in // 2):
        w_arrived(2, lax.rem(partner + 2 * d, n_in))

    def finish_first(j, carry):
        finish(0, j)
        return carry

    lax.fori_loop(0, 2, finish_first, 0)
    turns = 2 * nz - 1

    def down_rest(j, carry):
        _, zz = owner(j % turns)

        @pl.when(inside(zz))
        def _():
            down(1 + j // turns, zz)

        return carry

    lax.fori_loop(0, (chunks - 1) * turns, down_rest, 0)
    lax.fori_loop(2, turns - 1, finish_first, 0)

    def finish_rest(j, carry):
        finish(1 + j // (turns - 1), j % (turns - 1))
        return carry

    lax.fori_loop(0, (chunks - 1) * (turns - 1), finish_rest, 0)
    for p in range(chunks):
        here = pl.ds(pl.multiple_of(columns_of(p) * 2 * width, 2 * width), 2 * width)
        for way in range(2):
            @pl.when(inside(z - (1 - 2 * way)))
            def _():
                sum_z(p, way, z).wait_recv()
                own_part[p, z] = own_part[p, z] + z_in[p, way, z].astype(F32)
        sum_x(p, z).wait_recv()
        out_ref[:, here] = (
            after[:, here].astype(F32) + (own_part[p, z] + x_in[p, z].astype(F32))).astype(BF16)

    @pl.when(o < n_out - 1)
    def _():
        kv_next().wait_send()

    for d in range(n_in // 2):
        kv_send(0, d).wait_send()
    for d in steps:
        kv_relay(0, d).wait_send()

    @pl.when(o > 0)
    def _():
        for d in range(n_in // 2):
            kv_send(1, d).wait_send()
        for d in steps:
            kv_relay(1, d).wait_send()

    for k in range(3):
        w_pair(k).wait_send()
        for d in steps:
            w_far(k, d).wait_send()
            w_relay(k, d).wait_send()
    for h in range(nz - 1):
        for way in range(2):
            step = 1 - 2 * way

            @pl.when(jnp.logical_and(inside(z - step * h), inside(z + step)))
            def _():
                tok_z(way, h).wait_send()
    for zz in range(nz):
        tok_x(zz).wait_send()
        for p in range(chunks):
            sum_x(p, zz).wait_send()

            @pl.when(z != zz)
            def _():
                sum_z(p, 0, zz).wait_send()


def per_device(n_out, n_in, resid, queries, keyvals, piece_order, out_proj, mlp_gain, w_gate, w_up, w_down):
    rows, model = resid.shape
    units = w_gate.shape[1]
    nz, chunks = n_out // 2, n_in // 2
    dma = pltpu.SemaphoreType.DMA
    vmem = pl.BlockSpec(memory_space=pltpu.VMEM)
    hbm = pl.BlockSpec(memory_space=pl.ANY)
    return pl.pallas_call(
        functools.partial(layer_kernel, n_out, n_in),
        out_shape=jax.ShapeDtypeStruct(resid.shape, BF16),
        in_specs=[pl.BlockSpec(memory_space=pltpu.SMEM)] + [vmem] * 5 + [hbm] * 3,
        out_specs=vmem,
        scratch_shapes=[
            pltpu.VMEM((2 * n_in * rows, keyvals.shape[1]), BF16),
            pltpu.VMEM((model, units), BF16),
            pltpu.VMEM((model, units), BF16),
            pltpu.VMEM((n_in,) + w_down.shape, BF16),
            pltpu.VMEM((n_out * rows, model), BF16),
            pltpu.VMEM((rows, model), BF16),
            pltpu.VMEM((n_out * rows, units), BF16),
            pltpu.VMEM((chunks, nz, rows, model // chunks), BF16),
            pltpu.VMEM((chunks, nz, rows, model // chunks), BF16),
            pltpu.VMEM((chunks, nz, rows, model // chunks), F32),
            pltpu.VMEM((chunks, nz, rows, model // chunks), BF16),
            pltpu.VMEM((chunks, 2, nz, rows, model // chunks), BF16),
            dma(()), dma(()), dma((2, n_in)), dma((2, n_in)),
            dma((3,)), dma((3,)), dma((3, n_in)), dma((3, n_in)), dma((3, n_in)),
            dma((2, nz)), dma((2, nz)), dma((nz,)), dma((nz,)),
            dma((chunks, nz)), dma((chunks, nz)), dma((chunks, nz)), dma((chunks, 2, nz)),
        ],
        compiler_params=pltpu.CompilerParams(
            collective_id=0, has_side_effects=True, vmem_limit_bytes=60000 * 1024
        ),
        name="layer",
    )(piece_order, resid, queries, keyvals, out_proj, mlp_gain.reshape(1, -1), w_gate, w_up, w_down)


def solution(mesh):
    placed = (
        P(("outer", "inner"), None),
        P(("outer", "inner"), None),
        P(("outer", "inner"), None),
        P(),
        P(),
        P(),
        P("inner", "outer"),
        P("inner", "outer"),
        P("outer", "inner"),
    )
    return jax.shard_map(
        functools.partial(per_device, mesh.shape["outer"], mesh.shape["inner"]),
        mesh=mesh,
        in_specs=placed,
        out_specs=P(("outer", "inner"), None),
        check_vma=False,
    )
```

```python
import functools

import jax
import jax.numpy as jnp
from jax import lax
from jax.experimental import pallas as pl
from jax.experimental.pallas import tpu as pltpu
from jax.sharding import PartitionSpec as P

MESH = pl.DeviceIdType.MESH
F32 = jnp.float32
BF16 = jnp.bfloat16
EPS = 1e-05


def layer_kernel(
    n_out, n_in,
    order_ref, resid_ref, query_ref, kv_ref, proj_ref, gain_ref, wg_ref, wu_ref, wd_ref,
    out_ref,
    kv_all, wg, wu, wd, tok, after, hidden, x_out, x_in, own_part, z_out, z_in,
    kv_loc, kv_snd, kv_relay_snd, kv_rcv, w_loc, w_pair_snd, w_snd, w_relay_snd, w_rcv,
    z_snd, z_rcv, x_snd, x_rcv, rx_snd, rx_rcv, rz_snd, rz_rcv,
):
    o = lax.axis_index("outer")
    i = lax.axis_index("inner")
    nz = n_out // 2
    z, x = o // 2, o % 2
    core = i % 2
    x_peer = (z * 2 + 1 - x, i)
    core_peer = (o, i + 1 - 2 * core)
    rows = resid_ref.shape[0]
    head = kv_ref.shape[1] // 2
    heads = query_ref.shape[1] // head
    pieces = order_ref.shape[0]
    block = n_in * rows
    span = block // pieces
    depth = wg_ref.shape[0]

    def remote(src, dst, ssem, rsem, device):
        return pltpu.make_async_remote_copy(
            src_ref=src, dst_ref=dst, send_sem=ssem, recv_sem=rsem,
            device_id=device, device_id_type=MESH,
        )

    barrier = pltpu.get_barrier_semaphore()
    after_o, before_o = lax.rem(o + 1, n_out), lax.rem(o + n_out - 1, n_out)
    count = 0
    for d in range(1, n_in):
        pl.semaphore_signal(barrier, inc=1, device_id=(o, lax.rem(i + d, n_in)), device_id_type=MESH)
        count += 1
    for d in range(n_in // 2):
        for there in (after_o, before_o):
            pl.semaphore_signal(
                barrier, inc=1, device_id=(there, lax.rem(i + 2 * d, n_in)), device_id_type=MESH)
            count += 1
    for d in range(1, nz):
        pl.semaphore_signal(
            barrier, inc=1, device_id=(lax.rem(z + d, nz) * 2 + x, i), device_id_type=MESH)
        count += 1
    pl.semaphore_signal(barrier, inc=1, device_id=x_peer, device_id_type=MESH)
    count += 1
    pl.semaphore_wait(barrier, count)

    own_rows = pl.ds(pl.multiple_of(i * rows, rows), rows)
    kv_copy = pltpu.make_async_copy(kv_ref, kv_all.at[own_rows], kv_loc)
    kv_copy.start()

    steps = range(1, n_in // 2)

    def kv_slot(part, q):
        return kv_all.at[pl.ds(pl.multiple_of(part * block + q * rows, rows), rows)]

    def kv_send(part, d):
        return remote(kv_ref, kv_slot(part, i), kv_snd.at[part, d], kv_rcv.at[part, i],
                      (after_o if part else o, lax.rem(i + 2 * d, n_in)))

    def kv_relay(part, d):
        q = lax.rem(i + n_in - 2 * d, n_in)
        src = kv_ref if part == 0 and d == 0 else kv_slot(part, q)
        return remote(src, kv_slot(part, q), kv_relay_snd.at[part, d], kv_rcv.at[part, q], core_peer)

    def kv_arrived(part, q):
        here = kv_slot(part, q)
        remote(here, here, kv_relay_snd.at[part, 0], kv_rcv.at[part, q], core_peer).wait_recv()

    for d in steps:
        kv_send(0, d).start()

    @pl.when(o < n_out - 1)
    def _():
        for d in range(n_in // 2):
            kv_send(1, d).start()

    kv_relay(0, 0).start()

    def slot(k, q):
        if k == 2:
            return wd.at[q]
        full = wg if k == 0 else wu
        return full.at[pl.ds(pl.multiple_of(q * depth, depth), depth)]

    srcs = (wg_ref, wu_ref, wd_ref)
    def w_far(k, d):
        return remote(srcs[k], slot(k, i), w_snd.at[k, d], w_rcv.at[k, i],
                      (o, lax.rem(i + 2 * d, n_in)))

    def w_pair(k):
        return remote(srcs[k], slot(k, i), w_pair_snd.at[k], w_rcv.at[k, i], core_peer)

    def w_arrived(k, q):
        remote(slot(k, q), slot(k, q), w_pair_snd.at[k], w_rcv.at[k, q], core_peer).wait_recv()

    def w_relay(k, d):
        q = lax.rem(i + n_in - 2 * d, n_in)
        return remote(slot(k, q), slot(k, q), w_relay_snd.at[k, d], w_rcv.at[k, q], core_peer)

    def w_local(k):
        return pltpu.make_async_copy(srcs[k], slot(k, i), w_loc.at[k])

    for k in range(3):
        for d in steps:
            w_far(k, d).start()
    for k in range(3):
        w_pair(k).start()
        w_local(k).start()

    def relay_weight(k):
        for d in steps:
            w_arrived(k, lax.rem(i + n_in - 2 * d, n_in))
            w_relay(k, d).start()

    def weight_ready(k):
        w_local(k).wait()
        for d in range(n_in // 2):
            w_arrived(k, lax.rem(partner + 2 * d, n_in))

    lane = lax.broadcasted_iota(jnp.int32, (rows, block), 1)
    key_pos = jnp.zeros((rows, block), jnp.int32)
    for p in range(pieces):
        key_pos = jnp.where(lane // span == p, order_ref[p] * span + lane % span, key_pos)
    row = lax.broadcasted_iota(jnp.int32, (rows, block), 0)
    query_pos = jnp.zeros((rows, block), jnp.int32)
    for p in range(rows // span):
        query_pos = jnp.where(
            row // span == p, order_ref[i * (rows // span) + p] * span + row % span, query_pos)
    own_visible = key_pos <= query_pos
    before_visible = (jnp.zeros((rows, block), jnp.int32) + o) > 0

    @pl.when(o == 0)
    def _():
        kv_all[block:, :] = jnp.zeros((block, 2 * head), BF16)

    for d in steps:
        kv_arrived(0, lax.rem(i + n_in - 2 * d, n_in))
        kv_relay(0, d).start()

    @pl.when(o > 0)
    def _():
        for d in range(n_in // 2):
            kv_arrived(1, lax.rem(i + n_in - 2 * d, n_in))
            kv_relay(1, d).start()

    partner = i + 1 - 2 * core
    kv_copy.wait()
    for d in range(n_in // 2):
        kv_arrived(0, lax.rem(partner + 2 * d, n_in))

    @pl.when(o > 0)
    def _():
        for d in range(n_in // 2):
            kv_arrived(1, lax.rem(partner + 2 * d, n_in))

    parts = []
    nt = (((1,), (1,)), ((), ()))
    for h in range(heads):
        query = query_ref[:, h * head:(h + 1) * head]
        own_score = lax.dot_general(
            query, kv_all[:block, :head], nt, preferred_element_type=F32) * head ** (-0.5)
        before_score = lax.dot_general(
            query, kv_all[block:, :head], nt, preferred_element_type=F32) * head ** (-0.5)
        own_score = jnp.where(own_visible, own_score, -1e30)
        before_score = jnp.where(before_visible, before_score, -1e30)
        top = jnp.maximum(
            jnp.max(own_score, axis=1, keepdims=True), jnp.max(before_score, axis=1, keepdims=True))
        own_w = jnp.where(own_visible, jnp.exp(own_score - top), 0.0)
        before_w = jnp.where(before_visible, jnp.exp(before_score - top), 0.0)
        total = jnp.sum(own_w, axis=1, keepdims=True) + jnp.sum(before_w, axis=1, keepdims=True)
        mixed = jnp.dot(own_w.astype(BF16), kv_all[:block, head:], preferred_element_type=F32)
        mixed += jnp.dot(before_w.astype(BF16), kv_all[block:, head:], preferred_element_type=F32)
        parts.append((mixed / total).astype(BF16))
    attended = jnp.concatenate(parts, axis=1)
    after_attn = (
        resid_ref[...].astype(F32) + jnp.dot(attended, proj_ref[...], preferred_element_type=F32)
    ).astype(BF16)
    after[...] = after_attn
    wide = after_attn.astype(F32)
    normed = wide * lax.rsqrt(jnp.mean(wide * wide, axis=1, keepdims=True) + EPS) * gain_ref[...]

    def tok_rows(zz, xx):
        return tok.at[pl.ds(pl.multiple_of((zz * 2 + xx) * rows, rows), rows)]

    tok_rows(z, x)[...] = normed.astype(BF16)

    def z_device(zz):
        return (zz * 2 + x, i)

    def inside(zz):
        return jnp.logical_and(zz >= 0, zz < nz)

    def tok_z(way, h):
        step = 1 - 2 * way
        here = tok_rows(z - step * h, x)
        return remote(here, here, z_snd.at[way, h], z_rcv.at[way, h], z_device(z + step))

    def tok_z_arrived(way, h):
        here = tok_rows(z - (1 - 2 * way) * (h + 1), x)
        remote(here, here, z_snd.at[way, h], z_rcv.at[way, h], x_peer).wait_recv()

    def tok_x(zz):
        here = tok_rows(zz, x)
        return remote(here, here, x_snd.at[zz], x_rcv.at[zz], x_peer)

    def tok_x_arrived(zz):
        here = tok_rows(zz, 1 - x)
        remote(here, here, x_snd.at[zz], x_rcv.at[zz], x_peer).wait_recv()

    for way in range(2):
        @pl.when(inside(z + 1 - 2 * way))
        def _():
            tok_z(way, 0).start()
    tok_x(z).start()
    for h in range(nz - 1):
        for way in range(2):
            step = 1 - 2 * way
            source = z - step * (h + 1)

            @pl.when(inside(source))
            def _():
                tok_z_arrived(way, h)

                @pl.when(inside(z + step))
                def _():
                    tok_z(way, h + 1).start()

                tok_x(source).start()
        if h < 2:
            relay_weight(h)
    for k in range(min(nz - 1, 2), 2):
        relay_weight(k)
    weight_ready(0)
    weight_ready(1)

    chunks = n_in // 2
    width = wd_ref.shape[1]

    def columns_of(p):
        return lax.rem(i // 2 + chunks - p, chunks)

    def sum_x(p, zz):
        return remote(x_out.at[p, zz], x_in.at[p, zz], rx_snd.at[p, zz], rx_rcv.at[p, zz], x_peer)

    def sum_z(p, way, zz):
        step = jnp.where(inside(z + 1 - 2 * way), 1 - 2 * way, 0)
        return remote(z_out.at[p, zz], z_in.at[p, way, zz], rz_snd.at[p, zz], rz_rcv.at[p, way, zz],
                      z_device(z + step))

    def down(p, zz):
        def half(xx):
            return hidden[pl.ds(pl.multiple_of((zz * 2 + xx) * rows, rows), rows), :]

        both = jnp.concatenate([half(1 - x), half(x)], axis=0)
        for q in range(2):
            part = jnp.dot(both, wd[2 * columns_of(p) + q], preferred_element_type=F32)
            x_out[p, zz, :, q * width:(q + 1) * width] = part[:rows].astype(BF16)
            own_part[p, zz, :, q * width:(q + 1) * width] = part[rows:]
        sum_x(p, zz).start()

    def owner(j):
        way = j % 2
        return way, z + (nz - 1 - j // 2) * (1 - 2 * way)

    def finish(p, j):
        way, zz = owner(j)
        more = inside(z - (1 - 2 * way))

        @pl.when(inside(zz))
        def _():
            sum_x(p, zz).wait_recv()

            @pl.when(more)
            def _():
                sum_z(p, way, zz).wait_recv()
                z_out[p, zz] = (
                    own_part[p, zz] + x_in[p, zz].astype(F32) + z_in[p, way, zz].astype(F32)
                ).astype(BF16)

            @pl.when(jnp.logical_not(more))
            def _():
                z_out[p, zz] = (own_part[p, zz] + x_in[p, zz].astype(F32)).astype(BF16)

            sum_z(p, way, zz).start()

    w_local(2).wait()
    w_arrived(2, partner)

    def hidden_step(j, carry):
        zz = z + ((j + 1) // 2) * (1 - 2 * (j % 2))

        @pl.when(inside(zz))
        def _():
            tok_x_arrived(zz)
            here = pl.ds(pl.multiple_of(zz * 2 * rows, 2 * rows), 2 * rows)
            tokens = tok[here, :]
            gate = jnp.dot(tokens, wg[...], preferred_element_type=F32)
            upward = jnp.dot(tokens, wu[...], preferred_element_type=F32)
            hidden[here, :] = (gate / (1.0 + jnp.exp(-gate)) * upward).astype(BF16)

            @pl.when(j == 0)
            def _():
                down(0, zz)

        return carry

    lax.fori_loop(0, 2 * nz - 1, hidden_step, 0)

    def down_first(j, carry):
        _, zz = owner(j)

        @pl.when(inside(zz))
        def _():
            down(0, zz)

        return carry

    lax.fori_loop(0, 2 * (nz - 1), down_first, 0)
    relay_weight(2)
    for d in range(1, n_in // 2):
        w_arrived(2, lax.rem(partner + 2 * d, n_in))

    def finish_first(j, carry):
        finish(0, j)
        return carry

    lax.fori_loop(0, 2, finish_first, 0)
    turns = 2 * nz - 1

    def down_rest(j, carry):
        _, zz = owner(j % turns)

        @pl.when(inside(zz))
        def _():
            down(1 + j // turns, zz)

        return carry

    lax.fori_loop(0, (chunks - 1) * turns, down_rest, 0)
    lax.fori_loop(2, turns - 1, finish_first, 0)

    def finish_rest(j, carry):
        finish(1 + j // (turns - 1), j % (turns - 1))
        return carry

    lax.fori_loop(0, (chunks - 1) * (turns - 1), finish_rest, 0)
    for p in range(chunks):
        here = pl.ds(pl.multiple_of(columns_of(p) * 2 * width, 2 * width), 2 * width)
        for way in range(2):
            @pl.when(inside(z - (1 - 2 * way)))
            def _():
                sum_z(p, way, z).wait_recv()
                own_part[p, z] = own_part[p, z] + z_in[p, way, z].astype(F32)
        sum_x(p, z).wait_recv()
        out_ref[:, here] = (
            after[:, here].astype(F32) + (own_part[p, z] + x_in[p, z].astype(F32))).astype(BF16)

    for d in steps:
        kv_send(0, d).wait_send()
    for d in range(n_in // 2):
        kv_relay(0, d).wait_send()

    @pl.when(o < n_out - 1)
    def _():
        for d in range(n_in // 2):
            kv_send(1, d).wait_send()

    @pl.when(o > 0)
    def _():
        for d in range(n_in // 2):
            kv_relay(1, d).wait_send()

    for k in range(3):
        w_pair(k).wait_send()
        for d in steps:
            w_far(k, d).wait_send()
            w_relay(k, d).wait_send()
    for h in range(nz - 1):
        for way in range(2):
            step = 1 - 2 * way

            @pl.when(jnp.logical_and(inside(z - step * h), inside(z + step)))
            def _():
                tok_z(way, h).wait_send()
    for zz in range(nz):
        tok_x(zz).wait_send()
        for p in range(chunks):
            sum_x(p, zz).wait_send()

            @pl.when(z != zz)
            def _():
                sum_z(p, 0, zz).wait_send()


def per_device(n_out, n_in, resid, queries, keyvals, piece_order, out_proj, mlp_gain, w_gate, w_up, w_down):
    rows, model = resid.shape
    units = w_gate.shape[1]
    nz, chunks = n_out // 2, n_in // 2
    dma = pltpu.SemaphoreType.DMA
    vmem = pl.BlockSpec(memory_space=pltpu.VMEM)
    hbm = pl.BlockSpec(memory_space=pl.ANY)
    return pl.pallas_call(
        functools.partial(layer_kernel, n_out, n_in),
        out_shape=jax.ShapeDtypeStruct(resid.shape, BF16),
        in_specs=[pl.BlockSpec(memory_space=pltpu.SMEM)] + [vmem] * 5 + [hbm] * 3,
        out_specs=vmem,
        scratch_shapes=[
            pltpu.VMEM((2 * n_in * rows, keyvals.shape[1]), BF16),
            pltpu.VMEM((model, units), BF16),
            pltpu.VMEM((model, units), BF16),
            pltpu.VMEM((n_in,) + w_down.shape, BF16),
            pltpu.VMEM((n_out * rows, model), BF16),
            pltpu.VMEM((rows, model), BF16),
            pltpu.VMEM((n_out * rows, units), BF16),
            pltpu.VMEM((chunks, nz, rows, model // chunks), BF16),
            pltpu.VMEM((chunks, nz, rows, model // chunks), BF16),
            pltpu.VMEM((chunks, nz, rows, model // chunks), F32),
            pltpu.VMEM((chunks, nz, rows, model // chunks), BF16),
            pltpu.VMEM((chunks, 2, nz, rows, model // chunks), BF16),
            dma(()), dma((2, n_in)), dma((2, n_in)), dma((2, n_in)),
            dma((3,)), dma((3,)), dma((3, n_in)), dma((3, n_in)), dma((3, n_in)),
            dma((2, nz)), dma((2, nz)), dma((nz,)), dma((nz,)),
            dma((chunks, nz)), dma((chunks, nz)), dma((chunks, nz)), dma((chunks, 2, nz)),
        ],
        compiler_params=pltpu.CompilerParams(
            collective_id=0, has_side_effects=True, vmem_limit_bytes=60000 * 1024
        ),
        name="layer",
    )(piece_order, resid, queries, keyvals, out_proj, mlp_gain.reshape(1, -1), w_gate, w_up, w_down)


def solution(mesh):
    placed = (
        P(("outer", "inner"), None),
        P(("outer", "inner"), None),
        P(("outer", "inner"), None),
        P(),
        P(),
        P(),
        P("inner", "outer"),
        P("inner", "outer"),
        P("outer", "inner"),
    )
    return jax.shard_map(
        functools.partial(per_device, mesh.shape["outer"], mesh.shape["inner"]),
        mesh=mesh,
        in_specs=placed,
        out_specs=P(("outer", "inner"), None),
        check_vma=False,
    )
```

```python
import functools

import jax
import jax.numpy as jnp
from jax import lax
from jax.experimental import pallas as pl
from jax.experimental.pallas import tpu as pltpu
from jax.sharding import PartitionSpec as P

MESH = pl.DeviceIdType.MESH
F32 = jnp.float32
BF16 = jnp.bfloat16
EPS = 1e-05


def layer_kernel(
    n_out, n_in,
    order_ref, resid_ref, query_ref, kv_ref, proj_ref, gain_ref, wg_ref, wu_ref, wd_ref,
    out_ref,
    kv_all, wg, wu, wd, tok, after, hidden, x_out, x_in, own_part, z_out, z_in,
    kv_loc, kv_snd, kv_relay_snd, kv_rcv, w_loc, w_pair_snd, w_snd, w_relay_snd, w_rcv,
    z_snd, z_rcv, g_snd, g_rcv, x_snd, x_rcv, rx_snd, rx_rcv, rz_snd, rz_rcv,
):
    o = lax.axis_index("outer")
    i = lax.axis_index("inner")
    nz = n_out // 2
    z, x = o // 2, o % 2
    core = i % 2
    x_peer = (z * 2 + 1 - x, i)
    core_peer = (o, i + 1 - 2 * core)
    rows = resid_ref.shape[0]
    head = kv_ref.shape[1] // 2
    heads = query_ref.shape[1] // head
    pieces = order_ref.shape[0]
    block = n_in * rows
    span = block // pieces
    depth = wg_ref.shape[0]

    def remote(src, dst, ssem, rsem, device):
        return pltpu.make_async_remote_copy(
            src_ref=src, dst_ref=dst, send_sem=ssem, recv_sem=rsem,
            device_id=device, device_id_type=MESH,
        )

    barrier = pltpu.get_barrier_semaphore()
    after_o, before_o = lax.rem(o + 1, n_out), lax.rem(o + n_out - 1, n_out)
    count = 0
    for d in range(1, n_in):
        pl.semaphore_signal(barrier, inc=1, device_id=(o, lax.rem(i + d, n_in)), device_id_type=MESH)
        count += 1
    for d in range(n_in // 2):
        for there in (after_o, before_o):
            pl.semaphore_signal(
                barrier, inc=1, device_id=(there, lax.rem(i + 2 * d, n_in)), device_id_type=MESH)
            count += 1
    for d in range(1, nz):
        pl.semaphore_signal(
            barrier, inc=1, device_id=(lax.rem(z + d, nz) * 2 + x, i), device_id_type=MESH)
        count += 1
    pl.semaphore_signal(barrier, inc=1, device_id=x_peer, device_id_type=MESH)
    count += 1
    pl.semaphore_wait(barrier, count)

    own_rows = pl.ds(pl.multiple_of(i * rows, rows), rows)
    kv_copy = pltpu.make_async_copy(kv_ref, kv_all.at[own_rows], kv_loc)
    kv_copy.start()

    steps = range(1, n_in // 2)

    def kv_slot(part, q):
        return kv_all.at[pl.ds(pl.multiple_of(part * block + q * rows, rows), rows)]

    def kv_send(part, d):
        return remote(kv_ref, kv_slot(part, i), kv_snd.at[part, d], kv_rcv.at[part, i],
                      (after_o if part else o, lax.rem(i + 2 * d, n_in)))

    def kv_relay(part, d):
        q = lax.rem(i + n_in - 2 * d, n_in)
        src = kv_ref if part == 0 and d == 0 else kv_slot(part, q)
        return remote(src, kv_slot(part, q), kv_relay_snd.at[part, d], kv_rcv.at[part, q], core_peer)

    def kv_arrived(part, q):
        here = kv_slot(part, q)
        remote(here, here, kv_relay_snd.at[part, 0], kv_rcv.at[part, q], core_peer).wait_recv()

    for d in steps:
        kv_send(0, d).start()

    @pl.when(o < n_out - 1)
    def _():
        for d in range(n_in // 2):
            kv_send(1, d).start()

    kv_relay(0, 0).start()

    def slot(k, q):
        if k == 2:
            return wd.at[q]
        full = wg if k == 0 else wu
        return full.at[pl.ds(pl.multiple_of(q * depth, depth), depth)]

    srcs = (wg_ref, wu_ref, wd_ref)
    def w_far(k, d):
        return remote(srcs[k], slot(k, i), w_snd.at[k, d], w_rcv.at[k, i],
                      (o, lax.rem(i + 2 * d, n_in)))

    def w_pair(k):
        return remote(srcs[k], slot(k, i), w_pair_snd.at[k], w_rcv.at[k, i], core_peer)

    def w_arrived(k, q):
        remote(slot(k, q), slot(k, q), w_pair_snd.at[k], w_rcv.at[k, q], core_peer).wait_recv()

    def w_relay(k, d):
        q = lax.rem(i + n_in - 2 * d, n_in)
        return remote(slot(k, q), slot(k, q), w_relay_snd.at[k, d], w_rcv.at[k, q], core_peer)

    def w_local(k):
        return pltpu.make_async_copy(srcs[k], slot(k, i), w_loc.at[k])

    for k in range(3):
        for d in steps:
            w_far(k, d).start()
    for k in range(3):
        w_pair(k).start()
        w_local(k).start()

    def relay_weight(k):
        for d in steps:
            w_arrived(k, lax.rem(i + n_in - 2 * d, n_in))
            w_relay(k, d).start()

    def weight_ready(k):
        w_local(k).wait()
        for d in range(n_in // 2):
            w_arrived(k, lax.rem(partner + 2 * d, n_in))

    lane = lax.broadcasted_iota(jnp.int32, (rows, block), 1)
    key_pos = jnp.zeros((rows, block), jnp.int32)
    for p in range(pieces):
        key_pos = jnp.where(lane // span == p, order_ref[p] * span + lane % span, key_pos)
    row = lax.broadcasted_iota(jnp.int32, (rows, block), 0)
    query_pos = jnp.zeros((rows, block), jnp.int32)
    for p in range(rows // span):
        query_pos = jnp.where(
            row // span == p, order_ref[i * (rows // span) + p] * span + row % span, query_pos)
    own_visible = key_pos <= query_pos
    before_visible = (jnp.zeros((rows, block), jnp.int32) + o) > 0

    @pl.when(o == 0)
    def _():
        kv_all[block:, :] = jnp.zeros((block, 2 * head), BF16)

    for d in steps:
        kv_arrived(0, lax.rem(i + n_in - 2 * d, n_in))
        kv_relay(0, d).start()

    @pl.when(o > 0)
    def _():
        for d in range(n_in // 2):
            kv_arrived(1, lax.rem(i + n_in - 2 * d, n_in))
            kv_relay(1, d).start()

    partner = i + 1 - 2 * core
    kv_copy.wait()
    for d in range(n_in // 2):
        kv_arrived(0, lax.rem(partner + 2 * d, n_in))

    @pl.when(o > 0)
    def _():
        for d in range(n_in // 2):
            kv_arrived(1, lax.rem(partner + 2 * d, n_in))

    parts = []
    nt = (((1,), (1,)), ((), ()))
    for h in range(heads):
        query = query_ref[:, h * head:(h + 1) * head]
        own_score = lax.dot_general(
            query, kv_all[:block, :head], nt, preferred_element_type=F32) * head ** (-0.5)
        before_score = lax.dot_general(
            query, kv_all[block:, :head], nt, preferred_element_type=F32) * head ** (-0.5)
        own_score = jnp.where(own_visible, own_score, -1e30)
        before_score = jnp.where(before_visible, before_score, -1e30)
        top = jnp.maximum(
            jnp.max(own_score, axis=1, keepdims=True), jnp.max(before_score, axis=1, keepdims=True))
        own_w = jnp.where(own_visible, jnp.exp(own_score - top), 0.0)
        before_w = jnp.where(before_visible, jnp.exp(before_score - top), 0.0)
        total = jnp.sum(own_w, axis=1, keepdims=True) + jnp.sum(before_w, axis=1, keepdims=True)
        mixed = jnp.dot(own_w.astype(BF16), kv_all[:block, head:], preferred_element_type=F32)
        mixed += jnp.dot(before_w.astype(BF16), kv_all[block:, head:], preferred_element_type=F32)
        parts.append((mixed / total).astype(BF16))
    attended = jnp.concatenate(parts, axis=1)
    after_attn = (
        resid_ref[...].astype(F32) + jnp.dot(attended, proj_ref[...], preferred_element_type=F32)
    ).astype(BF16)
    after[...] = after_attn
    wide = after_attn.astype(F32)
    normed = wide * lax.rsqrt(jnp.mean(wide * wide, axis=1, keepdims=True) + EPS) * gain_ref[...]

    def tok_rows(zz, xx):
        return tok.at[pl.ds(pl.multiple_of((zz * 2 + xx) * rows, rows), rows)]

    tok_rows(z, x)[...] = normed.astype(BF16)

    def z_device(zz):
        return (zz * 2 + x, i)

    def inside(zz):
        return jnp.logical_and(zz >= 0, zz < nz)

    def tok_z(way, h):
        step = 1 - 2 * way
        here = tok_rows(z - step * h, x)
        return remote(here, here, z_snd.at[way, h], z_rcv.at[way, h], z_device(z + step))

    def tok_z_arrived(way, h):
        here = tok_rows(z - (1 - 2 * way) * (h + 1), x)
        remote(here, here, z_snd.at[way, h], z_rcv.at[way, h], x_peer).wait_recv()

    keep = rows - rows // 4

    def tok_x_own(xx):
        here = tok_rows(z, xx)
        return remote(here, here, x_snd.at[z], x_rcv.at[z], x_peer)

    def tok_first(zz, xx):
        here = tok.at[pl.ds(pl.multiple_of((zz * 2 + xx) * rows, rows), keep)]
        return remote(here, here, x_snd.at[zz], x_rcv.at[zz], x_peer)

    def tok_last(way, h, hops, to):
        zz = z - (1 - 2 * way) * hops
        here = tok.at[pl.ds(pl.multiple_of((zz * 2 + 1 - x) * rows + keep, rows // 4), rows - keep)]
        return remote(here, here, g_snd.at[way, h], g_rcv.at[way, h], to)

    def last_hop(h):
        for way in range(2):
            step = 1 - 2 * way

            @pl.when(jnp.logical_and(inside(z - step * h), inside(z + step)))
            def _():
                tok_last(way, h, h, z_device(z + step)).start()

    def last_arrived(h):
        for way in range(2):
            @pl.when(inside(z - (1 - 2 * way) * (h + 1)))
            def _():
                tok_last(way, h, h + 1, x_peer).wait_recv()

    for way in range(2):
        @pl.when(inside(z + 1 - 2 * way))
        def _():
            tok_z(way, 0).start()
    tok_x_own(x).start()
    for h in range(nz - 1):
        for way in range(2):
            step = 1 - 2 * way
            source = z - step * (h + 1)

            @pl.when(inside(source))
            def _():
                tok_z_arrived(way, h)

                @pl.when(inside(z + step))
                def _():
                    tok_z(way, h + 1).start()

                tok_first(source, x).start()
        if h == 0:
            tok_x_own(1 - x).wait_recv()
        else:
            last_arrived(h - 1)
        last_hop(h)
        if h < 2:
            relay_weight(h)
    for k in range(min(nz - 1, 2), 2):
        relay_weight(k)
    weight_ready(0)
    weight_ready(1)

    chunks = n_in // 2
    width = wd_ref.shape[1]

    def columns_of(p):
        return lax.rem(i // 2 + chunks - p, chunks)

    def sum_x(p, zz):
        return remote(x_out.at[p, zz], x_in.at[p, zz], rx_snd.at[p, zz], rx_rcv.at[p, zz], x_peer)

    def sum_z(p, way, zz):
        step = jnp.where(inside(z + 1 - 2 * way), 1 - 2 * way, 0)
        return remote(z_out.at[p, zz], z_in.at[p, way, zz], rz_snd.at[p, zz], rz_rcv.at[p, way, zz],
                      z_device(z + step))

    def down(p, zz):
        def half(xx):
            return hidden[pl.ds(pl.multiple_of((zz * 2 + xx) * rows, rows), rows), :]

        both = jnp.concatenate([half(1 - x), half(x)], axis=0)
        for q in range(2):
            part = jnp.dot(both, wd[2 * columns_of(p) + q], preferred_element_type=F32)
            x_out[p, zz, :, q * width:(q + 1) * width] = part[:rows].astype(BF16)
            own_part[p, zz, :, q * width:(q + 1) * width] = part[rows:]
        sum_x(p, zz).start()

    def owner(j):
        way = j % 2
        return way, z + (nz - 1 - j // 2) * (1 - 2 * way)

    def finish(p, j):
        way, zz = owner(j)
        more = inside(z - (1 - 2 * way))

        @pl.when(inside(zz))
        def _():
            sum_x(p, zz).wait_recv()

            @pl.when(more)
            def _():
                sum_z(p, way, zz).wait_recv()
                z_out[p, zz] = (
                    own_part[p, zz] + x_in[p, zz].astype(F32) + z_in[p, way, zz].astype(F32)
                ).astype(BF16)

            @pl.when(jnp.logical_not(more))
            def _():
                z_out[p, zz] = (own_part[p, zz] + x_in[p, zz].astype(F32)).astype(BF16)

            sum_z(p, way, zz).start()

    w_local(2).wait()
    w_arrived(2, partner)

    def hidden_step(j, carry):
        zz = z + ((j + 1) // 2) * (1 - 2 * (j % 2))

        @pl.when(inside(zz))
        def _():
            @pl.when(j > 0)
            def _():
                tok_first(zz, 1 - x).wait_recv()

            @pl.when((j + 1) // 2 == nz - 1)
            def _():
                tok_last(1 - j % 2, nz - 2, nz - 1, x_peer).wait_recv()

            here = pl.ds(pl.multiple_of(zz * 2 * rows, 2 * rows), 2 * rows)
            tokens = tok[here, :]
            gate = jnp.dot(tokens, wg[...], preferred_element_type=F32)
            upward = jnp.dot(tokens, wu[...], preferred_element_type=F32)
            hidden[here, :] = (gate / (1.0 + jnp.exp(-gate)) * upward).astype(BF16)

            @pl.when(j == 0)
            def _():
                down(0, zz)

        return carry

    lax.fori_loop(0, 2 * nz - 1, hidden_step, 0)

    def down_first(j, carry):
        _, zz = owner(j)

        @pl.when(inside(zz))
        def _():
            down(0, zz)

        return carry

    lax.fori_loop(0, 2 * (nz - 1), down_first, 0)
    relay_weight(2)
    for d in range(1, n_in // 2):
        w_arrived(2, lax.rem(partner + 2 * d, n_in))

    def finish_first(j, carry):
        finish(0, j)
        return carry

    lax.fori_loop(0, 2, finish_first, 0)
    turns = 2 * nz - 1

    def down_rest(j, carry):
        _, zz = owner(j % turns)

        @pl.when(inside(zz))
        def _():
            down(1 + j // turns, zz)

        return carry

    lax.fori_loop(0, (chunks - 1) * turns, down_rest, 0)
    lax.fori_loop(2, turns - 1, finish_first, 0)

    def finish_rest(j, carry):
        finish(1 + j // (turns - 1), j % (turns - 1))
        return carry

    lax.fori_loop(0, (chunks - 1) * (turns - 1), finish_rest, 0)
    for p in range(chunks):
        here = pl.ds(pl.multiple_of(columns_of(p) * 2 * width, 2 * width), 2 * width)
        for way in range(2):
            @pl.when(inside(z - (1 - 2 * way)))
            def _():
                sum_z(p, way, z).wait_recv()
                own_part[p, z] = own_part[p, z] + z_in[p, way, z].astype(F32)
        sum_x(p, z).wait_recv()
        out_ref[:, here] = (
            after[:, here].astype(F32) + (own_part[p, z] + x_in[p, z].astype(F32))).astype(BF16)

    for d in steps:
        kv_send(0, d).wait_send()
    for d in range(n_in // 2):
        kv_relay(0, d).wait_send()

    @pl.when(o < n_out - 1)
    def _():
        for d in range(n_in // 2):
            kv_send(1, d).wait_send()

    @pl.when(o > 0)
    def _():
        for d in range(n_in // 2):
            kv_relay(1, d).wait_send()

    for k in range(3):
        w_pair(k).wait_send()
        for d in steps:
            w_far(k, d).wait_send()
            w_relay(k, d).wait_send()
    for h in range(nz - 1):
        for way in range(2):
            step = 1 - 2 * way

            @pl.when(jnp.logical_and(inside(z - step * h), inside(z + step)))
            def _():
                tok_z(way, h).wait_send()
                tok_last(way, h, h, x_peer).wait_send()
    for zz in range(nz):
        @pl.when(z == zz)
        def _():
            tok_x_own(x).wait_send()

        @pl.when(z != zz)
        def _():
            tok_first(zz, x).wait_send()

        for p in range(chunks):
            sum_x(p, zz).wait_send()

            @pl.when(z != zz)
            def _():
                sum_z(p, 0, zz).wait_send()


def per_device(n_out, n_in, resid, queries, keyvals, piece_order, out_proj, mlp_gain, w_gate, w_up, w_down):
    rows, model = resid.shape
    units = w_gate.shape[1]
    nz, chunks = n_out // 2, n_in // 2
    dma = pltpu.SemaphoreType.DMA
    vmem = pl.BlockSpec(memory_space=pltpu.VMEM)
    hbm = pl.BlockSpec(memory_space=pl.ANY)
    return pl.pallas_call(
        functools.partial(layer_kernel, n_out, n_in),
        out_shape=jax.ShapeDtypeStruct(resid.shape, BF16),
        in_specs=[pl.BlockSpec(memory_space=pltpu.SMEM)] + [vmem] * 5 + [hbm] * 3,
        out_specs=vmem,
        scratch_shapes=[
            pltpu.VMEM((2 * n_in * rows, keyvals.shape[1]), BF16),
            pltpu.VMEM((model, units), BF16),
            pltpu.VMEM((model, units), BF16),
            pltpu.VMEM((n_in,) + w_down.shape, BF16),
            pltpu.VMEM((n_out * rows, model), BF16),
            pltpu.VMEM((rows, model), BF16),
            pltpu.VMEM((n_out * rows, units), BF16),
            pltpu.VMEM((chunks, nz, rows, model // chunks), BF16),
            pltpu.VMEM((chunks, nz, rows, model // chunks), BF16),
            pltpu.VMEM((chunks, nz, rows, model // chunks), F32),
            pltpu.VMEM((chunks, nz, rows, model // chunks), BF16),
            pltpu.VMEM((chunks, 2, nz, rows, model // chunks), BF16),
            dma(()), dma((2, n_in)), dma((2, n_in)), dma((2, n_in)),
            dma((3,)), dma((3,)), dma((3, n_in)), dma((3, n_in)), dma((3, n_in)),
            dma((2, nz)), dma((2, nz)), dma((2, nz)), dma((2, nz)), dma((nz,)), dma((nz,)),
            dma((chunks, nz)), dma((chunks, nz)), dma((chunks, nz)), dma((chunks, 2, nz)),
        ],
        compiler_params=pltpu.CompilerParams(
            collective_id=0, has_side_effects=True, vmem_limit_bytes=60000 * 1024
        ),
        name="layer",
    )(piece_order, resid, queries, keyvals, out_proj, mlp_gain.reshape(1, -1), w_gate, w_up, w_down)


def solution(mesh):
    placed = (
        P(("outer", "inner"), None),
        P(("outer", "inner"), None),
        P(("outer", "inner"), None),
        P(),
        P(),
        P(),
        P("inner", "outer"),
        P("inner", "outer"),
        P("outer", "inner"),
    )
    return jax.shard_map(
        functools.partial(per_device, mesh.shape["outer"], mesh.shape["inner"]),
        mesh=mesh,
        in_specs=placed,
        out_specs=P(("outer", "inner"), None),
        check_vma=False,
    )
```
